32 devices in a mesh: group: 2 (over y), section: 4 (over z), span: 2 (over x), mp: 2 (over core).
Axes of the slice: x: 2, y: 2, z: 4, core: 2. Of those that a mesh axis runs over, the one named last changes fastest.
Arguments:
- queries: bfloat16 [8, 256, 4096], P(('group', 'section'), None, ('span', 'mp')), parts along dimension 0, may hold values from -5 to 5
- keys_values: bfloat16 [2, 8, 256, 4096], P(None, ('group', 'section'), None, ('span', 'mp')), parts along dimension 1, may hold values from -5 to 5
- latents: bfloat16 [8, 256, 5120], P(('group', 'section'), ('span', 'mp')), parts along dimension 0, may hold values from -6 to 6
- out_weight: bfloat16 [4096, 5120], P(('span', 'mp')), may hold values from -3 to 3
- gate_table: float32 [8, 5120], replicated, may hold values from 0.5 to 1.5
- level_index: int32 [8], P(('group', 'section')), parts along dimension 0, may hold values from 0 to 7
- pair_window: int32 [6], P('group'), parts along dimension 0, may hold values from 0 to 256
Outputs:
- shifted: bfloat16 [8, 256, 5120], P(('group', 'section'), ('span', 'mp')), parts along dimension 0
The draws below stay inside these ranges and needn't reach their ends.
There are 2 independent parts, one for each index of `group`. The reference program is written for one: setup_inputs(seed, part) draws one part's arguments, and reference() takes and returns one part's arrays. A program takes and returns all parts, laid end to end along the dimension named above; an argument that names none is the same for every part. Nothing has to cross between parts.
All inputs are finite; a program needn't handle non-finite values.
Results may differ from the reference program's by a relative error of at most 0.015.
Values may be sent and summed in bfloat16 or wider, within the bound.
A program may use at most 64 MiB of HBM per device.

```python
import math
import jax
import jax.numpy as jnp
from jax import lax

D = 5120
HD = 128
LEVELS = 8
SPAN_TOK = 256
NS = 4
HQ = 4096


def draw_triple(key):
    key_query, key_keys, key_values = jax.random.split(jax.random.fold_in(key, 7), 3)
    full_shape = (NS, SPAN_TOK, HQ)
    query_draw = jnp.clip(jax.random.normal(key_query, full_shape, jnp.float32), -5.0, 5.0)
    keys_draw = jnp.clip(jax.random.normal(key_keys, full_shape, jnp.float32), -5.0, 5.0)
    values_draw = jnp.clip(jax.random.normal(key_values, full_shape, jnp.float32), -5.0, 5.0)
    return (query_draw, keys_draw, values_draw)


def draw_queries(key, part):
    return draw_triple(key)[0].astype(jnp.bfloat16)


def draw_keys_values(key, part):
    triple = draw_triple(key)
    return jnp.stack([triple[1], triple[2]], 0).astype(jnp.bfloat16)


def draw_pair_window(key, part):
    key_rows, key_spot = jax.random.split(jax.random.fold_in(key, 11), 2)
    pair_count = NS - 1
    widths = jax.random.randint(key_rows, (pair_count,), 0, SPAN_TOK + 1)
    spot = jax.random.randint(key_spot, (), 0, pair_count)
    other = (spot + 1) % pair_count
    places = jnp.arange(pair_count, dtype=jnp.int32)
    widths = jnp.where(places == spot, SPAN_TOK, widths)
    widths = jnp.where(places == other, 0, widths)
    return widths.astype(jnp.int32)


def with_ends(values, rng, smallest, top_value):
    dims = values.shape
    index_at = [jax.random.randint(jax.random.fold_in(rng, axis), (), 0, dims[axis]) for axis in range(len(dims))]
    values = values.at[tuple(index_at)].set(smallest)
    longest = dims.index(max(dims))
    index_at[longest] = (index_at[longest] + 1) % dims[longest]
    return values.at[tuple(index_at)].set(top_value)


def block_scale(own_key, dims, pieces, least, top_value):
    factor_of, own = 1.0, jax.random.fold_in(own_key, 6)
    for position, parts in pieces:
        draws = jnp.exp(jax.random.uniform(jax.random.fold_in(own, position), (parts,), jnp.float32, least / len(pieces), top_value / len(pieces)))
        factor_of = factor_of * jnp.repeat(draws, dims[position] // parts).reshape([-1 if axis == position else 1 for axis in range(len(dims))])
    return factor_of


def gaussian(key, shape, scale, most, cuts=(), kind=jnp.bfloat16):
    loudness = block_scale(key, shape, cuts, -0.22, 0.18) if cuts else 1.0
    entries = jax.random.normal(key, shape, jnp.float32) * scale * loudness
    return jnp.minimum(jnp.maximum(entries, -most), most).astype(kind)


def setup_inputs(seed: int = 0, part: int = 0) -> dict:
    key_of = jax.random.split(jax.random.key(seed), 8)
    part_splits = jax.random.split(jax.random.fold_in(key_of[7], part), 8)
    return {
        "queries": draw_queries(jax.random.fold_in(jax.random.fold_in(key_of[7], part), 71), part),
        "keys_values": draw_keys_values(jax.random.fold_in(jax.random.fold_in(key_of[7], part), 71), part),
        "latents": gaussian(part_splits[2], (NS, SPAN_TOK, D), 1.0, 6.0, ((0, 4), (1, 4))),
        "out_weight": gaussian(key_of[3], (HQ, D), (max(HD // 32, 1)) ** -0.5, 3.0, ((0, 4),)),
        "gate_table": jnp.clip(jax.random.uniform(key_of[4], (LEVELS, D), jnp.float32, 0.5, 1.5), 0.5, 1.5),
        "level_index": with_ends(jax.random.randint(part_splits[5], (NS,), 0, LEVELS), jax.random.fold_in(part_splits[5], 1), 0, LEVELS - 1).astype(jnp.int32),
        "pair_window": draw_pair_window(jax.random.fold_in(jax.random.fold_in(key_of[7], part), 71), part),
    }


NEG_BIG = -1e+30

def reference(queries, keys_values, latents, out_weight, gate_table, level_index, pair_window):
    sections, span_tok, width_all = queries.shape
    head_count = width_all // HD
    score_scale = 1.0 / math.sqrt(HD)
    final_pair = sections - 2
    row_ids = jnp.arange(span_tok, dtype=jnp.int32)

    def one_section(section_id):
        prev_width = jnp.where(section_id > 0, pair_window[jnp.clip(section_id - 1, 0, final_pair)], 0)
        next_width = jnp.where(section_id < sections - 1, pair_window[jnp.clip(section_id, 0, final_pair)], 0)
        lower_id = jnp.clip(section_id - 1, 0, sections - 1)
        upper_id = jnp.clip(section_id + 1, 0, sections - 1)
        key_rows = jnp.concatenate([keys_values[0, lower_id], keys_values[0, section_id], keys_values[0, upper_id]], 0)
        value_rows = jnp.concatenate([keys_values[1, lower_id], keys_values[1, section_id], keys_values[1, upper_id]], 0)
        key_mask = jnp.concatenate([row_ids >= span_tok - prev_width, jnp.ones((span_tok,), bool), row_ids < next_width], 0)
        query_rows = queries[section_id]

        def one_head(head_id):
            col_start = head_id * HD
            query_head = lax.dynamic_slice_in_dim(query_rows, col_start, HD, 1)
            key_head = lax.dynamic_slice_in_dim(key_rows, col_start, HD, 1)
            value_head = lax.dynamic_slice_in_dim(value_rows, col_start, HD, 1)
            scores = jnp.dot(query_head, key_head.T, preferred_element_type=jnp.float32) * score_scale
            scores = jnp.where(key_mask[None, :], scores, NEG_BIG)
            row_max = lax.optimization_barrier(jnp.max(scores, axis=1, keepdims=True))
            probabilities = jnp.where(key_mask[None, :], jnp.exp(scores - row_max), 0.0)
            row_total = lax.optimization_barrier(jnp.sum(probabilities, axis=1, keepdims=True))
            weighted = jnp.dot(probabilities.astype(jnp.bfloat16), value_head, preferred_element_type=jnp.float32)
            return (weighted / row_total).astype(jnp.bfloat16)
        per_head = lax.map(one_head, jnp.arange(head_count, dtype=jnp.int32))
        attended = jnp.transpose(per_head, (1, 0, 2)).reshape(span_tok, width_all)
        projected = jnp.dot(attended, out_weight, preferred_element_type=jnp.float32)
        gate_row = gate_table[level_index[section_id]]
        return (latents[section_id].astype(jnp.float32) + gate_row[None, :] * projected).astype(jnp.bfloat16)
    updated = lax.map(one_section, jnp.arange(sections, dtype=jnp.int32))
    return jnp.roll(updated, 1, axis=0)
```

```python
import functools
import math

import jax
import jax.numpy as jnp
from jax import lax
from jax.experimental import pallas as pl
from jax.experimental.pallas import tpu as pltpu
from jax.sharding import PartitionSpec as P

HD = 128
NEG_BIG = -1e30
BLOCKS = 2
CHUNK = 512
LAG_MP = 3
LAG_SPAN = 7
LANES = 128


def fused(
    sections, spans, mps, blocks, chunk, lag_mp, lag_span,
    level_hbm, window_hbm, q_hbm, kv_hbm, lat_hbm, w_hbm, gate_hbm, out_hbm,
    q_buf, kv_buf, lat_buf, w_buf, gate_buf, q_in, o_out, o_in, lse_out, lse_in, own, lse_own, att, keep,
    send_mp, recv_mp, send_span, recv_span, send_next,
    level_ref, window_ref, load_sems, q_send, q_recv, o_send, o_recv, lse_send, lse_recv,
    mp_send, mp_recv, span_send, span_recv, next_send, next_recv, relay,
):
    s = lax.axis_index("section")
    x = lax.axis_index("span")
    m = lax.axis_index("mp")
    last = sections - 1
    owners, rows, width = q_buf.shape
    tokens = kv_buf.shape[1]
    heads = width // HD
    piece = rows // blocks
    group = owners * piece
    stat_rows = lse_out.shape[2]
    chunks = w_buf.shape[1] // chunk
    steps = blocks * chunks
    succ = lax.rem(s + 1, sections)
    pred = lax.rem(s + sections - 1, sections)

    barrier = pltpu.get_barrier_semaphore()

    @pl.when(s < last)
    def _():
        pl.semaphore_signal(barrier, 1, device_id={"section": succ})

    @pl.when(s > 0)
    def _():
        pl.semaphore_signal(barrier, 1, device_id={"section": pred})

    for j in range(1, mps):
        pl.semaphore_signal(barrier, 1, device_id={"mp": lax.rem(m + j, mps)})
    for i in range(1, spans):
        pl.semaphore_signal(barrier, 1, device_id={"span": lax.rem(x + i, spans)})
    others = mps - 1 + spans - 1

    windows = pltpu.make_async_copy(window_hbm, window_ref, load_sems.at[6])
    loads = [
        pltpu.make_async_copy(q_hbm, q_buf, load_sems.at[0]),
        pltpu.make_async_copy(kv_hbm.at[:, 0], kv_buf, load_sems.at[1]),
        pltpu.make_async_copy(lat_hbm.at[0], lat_buf, load_sems.at[2]),
        pltpu.make_async_copy(gate_hbm, gate_buf, load_sems.at[3]),
        pltpu.make_async_copy(w_hbm, w_buf, load_sems.at[4]),
        pltpu.make_async_copy(level_hbm, level_ref, load_sems.at[5]),
    ]

    @pl.when((s > 0) & (s < last))
    def _():
        pl.semaphore_wait(barrier, others + 2)

    @pl.when((s == 0) | (s == last))
    def _():
        pl.semaphore_wait(barrier, others + 1)

    def head_cols(h):
        return pl.ds(pl.multiple_of(h * HD, HD), HD)

    def chunk_cols(c):
        return pl.ds(pl.multiple_of(c * chunk, chunk), chunk)

    def piece_rows(b):
        return pl.ds(pl.multiple_of(b * piece, piece), piece)

    def to_side(side, src, dst, send, recv):
        return pltpu.make_async_remote_copy(
            src, dst, send, recv, device_id={"section": succ if side == 0 else pred}
        )

    def ask(side, b, h):
        return to_side(
            side, q_hbm.at[:, piece_rows(b), head_cols(h)], q_in.at[side, b, :, :, head_cols(h)],
            q_send.at[side, b, h], q_recv.at[side, b, h],
        )

    def reply(side, b, h):
        return to_side(
            side, o_out.at[1 - side, b, h], o_in.at[side, b, h], o_send.at[side, b, h], o_recv.at[side, b, h]
        )

    def reply_lse(side, b):
        return to_side(
            side, lse_out.at[1 - side, b], lse_in.at[side, b, pl.ds(0, stat_rows)],
            lse_send.at[side, b], lse_recv.at[side, b],
        )

    sends_to = [s < last, s > 0]
    hears_from = [s > 0, s < last]

    for b in range(blocks):
        @pl.loop(0, heads)
        def _(h):
            for side in range(2):
                @pl.when(sends_to[side])
                def _():
                    ask(side, b, h).start()

    windows.start()
    for load in loads:
        load.start()

    @pl.when(s == 0)
    def _():
        pl.semaphore_signal(relay, 1, device_id={"section": succ})

    lse_own[...] = jnp.zeros_like(lse_own)
    for side in range(2):
        lse_in[side, :, stat_rows:] = jnp.full((blocks, LANES - stat_rows, group), NEG_BIG, jnp.float32)

        @pl.when(jnp.logical_not(hears_from[side]))
        def _():
            lse_in[side, :, :stat_rows] = jnp.full((blocks, stat_rows, group), NEG_BIG, jnp.float32)
            o_in[side] = jnp.zeros(o_in.shape[1:], o_in.dtype)

    windows.wait()
    pairs = window_ref.shape[0]
    w_lo = jnp.where(s > 0, window_ref[jnp.clip(s - 1, 0, pairs - 1)], 0)
    w_hi = jnp.where(s < last, window_ref[jnp.clip(s, 0, pairs - 1)], 0)
    scale = 1.0 / math.sqrt(HD)
    loads[0].wait()
    loads[1].wait()

    def attend(q, h, mask):
        cols = head_cols(h)
        scores = lax.dot_general(
            q, kv_buf[0, :, cols], (((1,), (1,)), ((), ())), preferred_element_type=jnp.float32
        ) * scale
        if mask is not None:
            scores = jnp.where(mask, scores, NEG_BIG)
        top = jnp.max(scores, axis=1, keepdims=True)
        probs = jnp.exp(scores - top)
        total = jnp.sum(probs, axis=1, keepdims=True)
        weighted = jnp.dot(probs.astype(jnp.bfloat16), kv_buf[1, :, cols], preferred_element_type=jnp.float32)
        return weighted * (1.0 / total), top + jnp.log(total)

    @pl.loop(0, heads)
    def _(h):
        cols = head_cols(h)
        lane = lax.broadcasted_iota(jnp.int32, (1, LANES), 1)
        for b in range(blocks):
            q = q_buf[:, piece_rows(b), cols].reshape(group, HD)
            value, lse = attend(q, h, None)
            own[b, :, cols] = value
            lse_own[b] = jnp.where(lane == h, lse, lse_own[b])

    lane = lax.broadcasted_iota(jnp.int32, (1, LANES), 1)
    key_ids = lax.broadcasted_iota(jnp.int32, (2 * group, tokens), 1)
    from_before = lax.broadcasted_iota(jnp.int32, (2 * group, tokens), 0) < group
    mask = jnp.where(from_before, key_ids, tokens - 1 - key_ids) < jnp.where(from_before, w_lo, w_hi)
    for b in range(blocks):
        def one_head(h, stats):
            for side in range(2):
                @pl.when(hears_from[side])
                def _():
                    ask(side, b, h).wait_recv()
            q = q_in[:, b, :, :, head_cols(h)].reshape(2 * group, HD)
            value, lse = attend(q, h, mask)
            value = value.astype(jnp.bfloat16).reshape(2, group, HD)
            for side in range(2):
                o_out[side, b, h] = value[side]
            for side in range(2):
                @pl.when(sends_to[side])
                def _():
                    reply(side, b, h).start()
            return jnp.where(lane == h, lse, stats)

        stats = lax.fori_loop(0, heads, one_head, jnp.zeros((2 * group, LANES), jnp.float32))
        for side in range(2):
            lse_out[side, b] = stats[side * group:(side + 1) * group].T[:stat_rows]
        for side in range(2):
            @pl.when(sends_to[side])
            def _():
                reply_lse(side, b).start()

    @pl.when((s > 0) & (s < last))
    def _():
        pl.semaphore_wait(relay, 1)
        pl.semaphore_signal(relay, 1, device_id={"section": succ})

    @pl.when(s == last)
    def _():
        pl.semaphore_wait(relay, 1)

    for load in loads[2:]:
        load.wait()
    level = level_ref[0]

    def to_mp(j, t):
        return pltpu.make_async_remote_copy(
            send_mp.at[j - 1, t], recv_mp.at[j - 1, t], mp_send.at[j - 1, t], mp_recv.at[j - 1, t],
            device_id={"mp": lax.rem(m + j, mps)},
        )

    def to_span(i, t):
        return pltpu.make_async_remote_copy(
            send_span.at[i - 1, t], recv_span.at[i - 1, t],
            span_send.at[i - 1, t], span_recv.at[i - 1, t],
            device_id={"span": lax.rem(x + i, spans)},
        )

    def to_next(t):
        return pltpu.make_async_remote_copy(
            send_next.at[t], out_hbm.at[0, piece_rows(t // chunks), chunk_cols(t % chunks)],
            next_send.at[t], next_recv.at[t], device_id={"section": succ},
        )

    def combine(b):
        @pl.loop(0, heads)
        def _(h):
            for side in range(2):
                @pl.when(hears_from[side])
                def _():
                    reply(side, b, h).wait_recv()

        for side in range(2):
            @pl.when(hears_from[side])
            def _():
                reply_lse(side, b).wait_recv()

        parts = [lse_own[b], lse_in[0, b].T, lse_in[1, b].T]
        top = jnp.maximum(jnp.maximum(parts[0], parts[1]), parts[2])
        parts = [jnp.exp(part - top) for part in parts]
        total = 1.0 / (parts[0] + parts[1] + parts[2])
        parts = [part * total for part in parts]
        for h in range(heads):
            cols = slice(h * HD, (h + 1) * HD)
            shares = [part[:, h:h + 1] for part in parts]
            result = own[b, :, cols] * shares[0]
            for side in range(2):
                result = result + o_in[side, b, h].astype(jnp.float32) * shares[side + 1]
            result = result.astype(jnp.bfloat16).reshape(spans, mps, piece, HD)
            for xb in range(spans):
                for mb in range(mps):
                    att[b, lax.rem(mb - m + mps, mps), lax.rem(xb - x + spans, spans), :, cols] = result[xb, mb]

    def project(t):
        part = jnp.dot(
            att[t // chunks].reshape(group, width), w_buf[:, chunk_cols(t % chunks)],
            preferred_element_type=jnp.float32,
        ).reshape(mps, spans, piece, chunk)
        for j in range(1, mps):
            send_mp[j - 1, t] = part[j].astype(jnp.bfloat16)
            to_mp(j, t).start()
        keep[t] = part[0]

    def reduce_mp(t):
        total = keep[t]
        for j in range(1, mps):
            to_mp(j, t).wait_recv()
            total = total + recv_mp[j - 1, t].astype(jnp.float32)
        for i in range(1, spans):
            send_span[i - 1, t] = total[i].astype(jnp.bfloat16)
            to_span(i, t).start()
        keep[t, 0] = total[0]

    def finish(t):
        total = keep[t, 0]
        for i in range(1, spans):
            to_span(i, t).wait_recv()
            total = total + recv_span[i - 1, t].astype(jnp.float32)
        table = gate_buf[:, chunk_cols(t % chunks)]
        level_ids = lax.broadcasted_iota(jnp.int32, table.shape, 0)
        gate = jnp.sum(jnp.where(level_ids == level, table, 0.0), axis=0, keepdims=True)
        updated = lat_buf[piece_rows(t // chunks), chunk_cols(t % chunks)].astype(jnp.float32) + gate * total
        send_next[t] = updated.astype(jnp.bfloat16)
        to_next(t).start()

    @pl.loop(0, steps + lag_span)
    def _(step):
        for b in range(blocks):
            @pl.when(step == b * chunks)
            def _():
                combine(b)

        @pl.when(step < steps)
        def _():
            project(step)

        @pl.when((step >= lag_mp) & (step < steps + lag_mp))
        def _():
            reduce_mp(step - lag_mp)

        @pl.when(step >= lag_span)
        def _():
            finish(step - lag_span)

    for b in range(blocks):
        @pl.loop(0, heads)
        def _(h):
            for side in range(2):
                @pl.when(sends_to[side])
                def _():
                    ask(side, b, h).wait_send()
                    reply(side, b, h).wait_send()

        for side in range(2):
            @pl.when(sends_to[side])
            def _():
                reply_lse(side, b).wait_send()

    @pl.loop(0, steps)
    def _(t):
        for j in range(1, mps):
            to_mp(j, t).wait_send()
        for i in range(1, spans):
            to_span(i, t).wait_send()
        to_next(t).wait()


def shards(sizes, queries, keys_values, latents, out_weight, gate_table, level_index, pair_window):
    sections, spans, mps = sizes
    tokens, width = queries.shape[1:]
    rows, model = latents.shape[1:]
    heads = width // HD
    owners = spans * mps
    blocks = BLOCKS
    piece = rows // blocks
    group = owners * piece
    stat_rows = -(-heads // 8) * 8
    chunk = CHUNK if model % CHUNK == 0 else HD
    steps = blocks * (model // chunk)
    bf16, f32 = jnp.bfloat16, jnp.float32
    dma = pltpu.SemaphoreType.DMA
    hbm = pl.BlockSpec(memory_space=pltpu.HBM)
    return pl.pallas_call(
        functools.partial(fused, sections, spans, mps, blocks, chunk, LAG_MP, LAG_SPAN),
        out_shape=jax.ShapeDtypeStruct(latents.shape, bf16),
        in_specs=[hbm, hbm, hbm, hbm, hbm, hbm, hbm],
        out_specs=hbm,
        scratch_shapes=[
            pltpu.VMEM((owners, rows, width), bf16),
            pltpu.VMEM((2, tokens, width), bf16),
            pltpu.VMEM((rows, model), bf16),
            pltpu.VMEM(out_weight.shape, bf16),
            pltpu.VMEM(gate_table.shape, f32),
            pltpu.VMEM((2, blocks, owners, piece, width), bf16),
            pltpu.VMEM((2, blocks, heads, group, HD), bf16),
            pltpu.VMEM((2, blocks, heads, group, HD), bf16),
            pltpu.VMEM((2, blocks, stat_rows, group), f32),
            pltpu.VMEM((2, blocks, LANES, group), f32),
            pltpu.VMEM((blocks, group, width), f32),
            pltpu.VMEM((blocks, group, LANES), f32),
            pltpu.VMEM((blocks, mps, spans, piece, width), bf16),
            pltpu.VMEM((steps, spans, piece, chunk), f32),
            pltpu.VMEM((mps - 1, steps, spans, piece, chunk), bf16),
            pltpu.VMEM((mps - 1, steps, spans, piece, chunk), bf16),
            pltpu.VMEM((spans - 1, steps, piece, chunk), bf16),
            pltpu.VMEM((spans - 1, steps, piece, chunk), bf16),
            pltpu.VMEM((steps, piece, chunk), bf16),
            pltpu.SMEM(level_index.shape, jnp.int32),
            pltpu.SMEM(pair_window.shape, jnp.int32),
            dma((7,)),
            dma((2, blocks, heads)), dma((2, blocks, heads)),
            dma((2, blocks, heads)), dma((2, blocks, heads)),
            dma((2, blocks)), dma((2, blocks)),
            dma((mps - 1, steps)), dma((mps - 1, steps)),
            dma((spans - 1, steps)), dma((spans - 1, steps)),
            dma((steps,)), dma((steps,)),
            pltpu.SemaphoreType.REGULAR,
        ],
        compiler_params=pltpu.CompilerParams(
            collective_id=0, has_side_effects=True, vmem_limit_bytes=60 * 1024 * 1024
        ),
    )(level_index, pair_window, queries.reshape(owners, rows, width), keys_values, latents, out_weight, gate_table)


def solution(mesh):
    sizes = (mesh.shape["section"], mesh.shape["span"], mesh.shape["mp"])
    in_specs = (
        P(("group", "section"), None, ("span", "mp")),
        P(None, ("group", "section"), None, ("span", "mp")),
        P(("group", "section"), ("span", "mp"), None),
        P(("span", "mp"), None),
        P(),
        P(("group", "section")),
        P("group"),
    )
    out_specs = P(("group", "section"), ("span", "mp"), None)
    return jax.shard_map(
        functools.partial(shards, sizes), mesh=mesh, in_specs=in_specs, out_specs=out_specs,
        check_vma=False,
    )
```

```python
import functools
import math

import jax
import jax.numpy as jnp
from jax import lax
from jax.experimental import pallas as pl
from jax.experimental.pallas import tpu as pltpu
from jax.sharding import PartitionSpec as P

HD = 128
NEG_BIG = -1e30
BLOCKS = 2
CHUNK = 512
LAG_MP = 2
LAG_SPAN = 6
LATE_STEP = 2
LANES = 128


def fused(
    sections, spans, mps, blocks, chunk, lag_mp, lag_span, late_step,
    level_hbm, window_hbm, q_hbm, kv_hbm, lat_hbm, w_hbm, gate_hbm, out_hbm,
    q_buf, kv_buf, lat_buf, w_buf, gate_buf, q_in, o_out, o_in, lse_out, lse_in, own, lse_own, stats, att, keep,
    send_mp, recv_mp, send_span, recv_span, send_next,
    level_ref, window_ref, load_sems, q_send, q_recv, o_send, o_recv, lse_send, lse_recv,
    mp_send, mp_recv, span_send, span_recv, next_send, next_recv, relay,
):
    s = lax.axis_index("section")
    x = lax.axis_index("span")
    m = lax.axis_index("mp")
    last = sections - 1
    owners, rows, width = q_buf.shape
    tokens = kv_buf.shape[1]
    heads = width // HD
    piece = rows // blocks
    group = owners * piece
    stat_rows = lse_out.shape[2]
    chunks = w_buf.shape[1] // chunk
    steps = blocks * chunks
    succ = lax.rem(s + 1, sections)
    pred = lax.rem(s + sections - 1, sections)

    barrier = pltpu.get_barrier_semaphore()

    @pl.when(s < last)
    def _():
        pl.semaphore_signal(barrier, 1, device_id={"section": succ})

    @pl.when(s > 0)
    def _():
        pl.semaphore_signal(barrier, 1, device_id={"section": pred})

    for j in range(1, mps):
        pl.semaphore_signal(barrier, 1, device_id={"mp": lax.rem(m + j, mps)})
    for i in range(1, spans):
        pl.semaphore_signal(barrier, 1, device_id={"span": lax.rem(x + i, spans)})
    others = mps - 1 + spans - 1

    windows = pltpu.make_async_copy(window_hbm, window_ref, load_sems.at[6])
    loads = [
        pltpu.make_async_copy(q_hbm, q_buf, load_sems.at[0]),
        pltpu.make_async_copy(kv_hbm.at[:, 0], kv_buf, load_sems.at[1]),
        pltpu.make_async_copy(lat_hbm.at[0], lat_buf, load_sems.at[2]),
        pltpu.make_async_copy(gate_hbm, gate_buf, load_sems.at[3]),
        pltpu.make_async_copy(w_hbm, w_buf, load_sems.at[4]),
        pltpu.make_async_copy(level_hbm, level_ref, load_sems.at[5]),
    ]

    windows.start()
    for load in loads:
        load.start()

    @pl.when((s > 0) & (s < last))
    def _():
        pl.semaphore_wait(barrier, others + 2)

    @pl.when((s == 0) | (s == last))
    def _():
        pl.semaphore_wait(barrier, others + 1)

    def head_cols(h):
        return pl.ds(pl.multiple_of(h * HD, HD), HD)

    def chunk_cols(c):
        return pl.ds(pl.multiple_of(c * chunk, chunk), chunk)

    def piece_rows(b):
        return pl.ds(pl.multiple_of(b * piece, piece), piece)

    def to_side(side, src, dst, send, recv):
        return pltpu.make_async_remote_copy(
            src, dst, send, recv, device_id={"section": succ if side == 0 else pred}
        )

    def ask(side, b, h):
        return to_side(
            side, q_hbm.at[:, piece_rows(b), head_cols(h)], q_in.at[side, b, :, :, head_cols(h)],
            q_send.at[side, b, h], q_recv.at[side, b, h],
        )

    def reply(side, b, h):
        return to_side(
            side, o_out.at[1 - side, b, h], o_in.at[side, b, h], o_send.at[side, b, h], o_recv.at[side, b, h]
        )

    def reply_lse(side, b):
        return to_side(
            side, lse_out.at[1 - side, b], lse_in.at[side, b, pl.ds(0, stat_rows)],
            lse_send.at[side, b], lse_recv.at[side, b],
        )

    sends_to = [s < last, s > 0]
    hears_from = [s > 0, s < last]

    def ask_all(b, first, end):
        @pl.loop(first, end)
        def _(h):
            for side in range(2):
                @pl.when(sends_to[side])
                def _():
                    ask(side, b, h).start()

    early = heads // 2
    late = heads - early
    ask_all(0, 0, heads)
    ask_all(1, 0, early)

    @pl.when(s == 0)
    def _():
        pl.semaphore_signal(relay, 1, device_id={"section": succ})

    lse_own[...] = jnp.zeros_like(lse_own)
    stats[...] = jnp.zeros_like(stats)
    for side in range(2):
        lse_in[side, :, stat_rows:] = jnp.full((blocks, LANES - stat_rows, group), NEG_BIG, jnp.float32)

        @pl.when(jnp.logical_not(hears_from[side]))
        def _():
            lse_in[side, :, :stat_rows] = jnp.full((blocks, stat_rows, group), NEG_BIG, jnp.float32)
            o_in[side] = jnp.zeros(o_in.shape[1:], o_in.dtype)

    windows.wait()
    pairs = window_ref.shape[0]
    w_lo = jnp.where(s > 0, window_ref[jnp.clip(s - 1, 0, pairs - 1)], 0)
    w_hi = jnp.where(s < last, window_ref[jnp.clip(s, 0, pairs - 1)], 0)
    scale = 1.0 / math.sqrt(HD)
    loads[0].wait()
    loads[1].wait()

    def attend(q, h, mask):
        cols = head_cols(h)
        scores = lax.dot_general(
            q, kv_buf[0, :, cols], (((1,), (1,)), ((), ())), preferred_element_type=jnp.float32
        ) * scale
        if mask is not None:
            scores = jnp.where(mask, scores, NEG_BIG)
        top = jnp.max(scores, axis=1, keepdims=True)
        probs = jnp.exp(scores - top)
        total = jnp.sum(probs, axis=1, keepdims=True)
        weighted = jnp.dot(probs.astype(jnp.bfloat16), kv_buf[1, :, cols], preferred_element_type=jnp.float32)
        return weighted * (1.0 / total), top + jnp.log(total)

    @pl.loop(0, heads)
    def _(h):
        cols = head_cols(h)
        lane = lax.broadcasted_iota(jnp.int32, (1, LANES), 1)
        for b in range(blocks):
            q = q_buf[:, piece_rows(b), cols].reshape(group, HD)
            value, lse = attend(q, h, None)
            own[b, :, cols] = value
            lse_own[b] = jnp.where(lane == h, lse, lse_own[b])

    def mask():
        key_ids = lax.broadcasted_iota(jnp.int32, (2 * group, tokens), 1)
        from_before = lax.broadcasted_iota(jnp.int32, (2 * group, tokens), 0) < group
        return jnp.where(from_before, key_ids, tokens - 1 - key_ids) < jnp.where(from_before, w_lo, w_hi)

    def answer(b, h):
        for side in range(2):
            @pl.when(hears_from[side])
            def _():
                ask(side, b, h).wait_recv()
        q = q_in[:, b, :, :, head_cols(h)].reshape(2 * group, HD)
        value, lse = attend(q, h, mask())
        value = value.astype(jnp.bfloat16).reshape(2, group, HD)
        for side in range(2):
            o_out[side, b, h] = value[side]
        for side in range(2):
            @pl.when(sends_to[side])
            def _():
                reply(side, b, h).start()
        stats[b] = jnp.where(lax.broadcasted_iota(jnp.int32, (1, LANES), 1) == h, lse, stats[b])

    def answer_lse(b):
        for side in range(2):
            lse_out[side, b] = stats[b, side * group:(side + 1) * group].T[:stat_rows]
        for side in range(2):
            @pl.when(sends_to[side])
            def _():
                reply_lse(side, b).start()

    @pl.loop(0, heads)
    def _(h):
        answer(0, h)

    answer_lse(0)
    ask_all(1, early, heads)

    @pl.loop(0, early)
    def _(h):
        answer(1, h)

    @pl.when((s > 0) & (s < last))
    def _():
        pl.semaphore_wait(relay, 1)
        pl.semaphore_signal(relay, 1, device_id={"section": succ})

    @pl.when(s == last)
    def _():
        pl.semaphore_wait(relay, 1)

    for load in loads[2:]:
        load.wait()
    level = level_ref[0]

    def to_mp(j, t):
        return pltpu.make_async_remote_copy(
            send_mp.at[j - 1, t], recv_mp.at[j - 1, t], mp_send.at[j - 1, t], mp_recv.at[j - 1, t],
            device_id={"mp": lax.rem(m + j, mps)},
        )

    def to_span(i, t):
        return pltpu.make_async_remote_copy(
            send_span.at[i - 1, t], recv_span.at[i - 1, t],
            span_send.at[i - 1, t], span_recv.at[i - 1, t],
            device_id={"span": lax.rem(x + i, spans)},
        )

    def to_next(t):
        return pltpu.make_async_remote_copy(
            send_next.at[t], out_hbm.at[0, piece_rows(t // chunks), chunk_cols(t % chunks)],
            next_send.at[t], next_recv.at[t], device_id={"section": succ},
        )

    def combine(b):
        @pl.loop(0, heads)
        def _(h):
            for side in range(2):
                @pl.when(hears_from[side])
                def _():
                    reply(side, b, h).wait_recv()

        for side in range(2):
            @pl.when(hears_from[side])
            def _():
                reply_lse(side, b).wait_recv()

        parts = [lse_own[b], lse_in[0, b].T, lse_in[1, b].T]
        top = jnp.maximum(jnp.maximum(parts[0], parts[1]), parts[2])
        parts = [jnp.exp(part - top) for part in parts]
        total = 1.0 / (parts[0] + parts[1] + parts[2])
        parts = [part * total for part in parts]
        for h in range(heads):
            cols = slice(h * HD, (h + 1) * HD)
            shares = [part[:, h:h + 1] for part in parts]
            result = own[b, :, cols] * shares[0]
            for side in range(2):
                result = result + o_in[side, b, h].astype(jnp.float32) * shares[side + 1]
            result = result.astype(jnp.bfloat16).reshape(spans, mps, piece, HD)
            for xb in range(spans):
                for mb in range(mps):
                    att[b, lax.rem(mb - m + mps, mps), lax.rem(xb - x + spans, spans), :, cols] = result[xb, mb]

    def project(t):
        part = jnp.dot(
            att[t // chunks].reshape(group, width), w_buf[:, chunk_cols(t % chunks)],
            preferred_element_type=jnp.float32,
        ).reshape(mps, spans, piece, chunk)
        for j in range(1, mps):
            send_mp[j - 1, t] = part[j].astype(jnp.bfloat16)
            to_mp(j, t).start()
        keep[t] = part[0]

    def reduce_mp(t):
        total = keep[t]
        for j in range(1, mps):
            to_mp(j, t).wait_recv()
            total = total + recv_mp[j - 1, t].astype(jnp.float32)
        for i in range(1, spans):
            send_span[i - 1, t] = total[i].astype(jnp.bfloat16)
            to_span(i, t).start()
        keep[t, 0] = total[0]

    def finish(t):
        total = keep[t, 0]
        for i in range(1, spans):
            to_span(i, t).wait_recv()
            total = total + recv_span[i - 1, t].astype(jnp.float32)
        table = gate_buf[:, chunk_cols(t % chunks)]
        level_ids = lax.broadcasted_iota(jnp.int32, table.shape, 0)
        gate = jnp.sum(jnp.where(level_ids == level, table, 0.0), axis=0, keepdims=True)
        updated = lat_buf[piece_rows(t // chunks), chunk_cols(t % chunks)].astype(jnp.float32) + gate * total
        send_next[t] = updated.astype(jnp.bfloat16)
        to_next(t).start()

    @pl.loop(0, steps + lag_span)
    def _(step):
        for b in range(blocks):
            @pl.when(step == b * chunks)
            def _():
                combine(b)

        @pl.when(step < steps)
        def _():
            project(step)

        @pl.when((step >= lag_mp) & (step < steps + lag_mp))
        def _():
            reduce_mp(step - lag_mp)

        @pl.when(step >= lag_span)
        def _():
            finish(step - lag_span)

        @pl.when((step >= late_step) & (step < late_step + late))
        def _():
            answer(1, early + step - late_step)

        @pl.when(step == late_step + late - 1)
        def _():
            answer_lse(1)

    for b in range(blocks):
        @pl.loop(0, heads)
        def _(h):
            for side in range(2):
                @pl.when(sends_to[side])
                def _():
                    ask(side, b, h).wait_send()
                    reply(side, b, h).wait_send()

        for side in range(2):
            @pl.when(sends_to[side])
            def _():
                reply_lse(side, b).wait_send()

    @pl.loop(0, steps)
    def _(t):
        for j in range(1, mps):
            to_mp(j, t).wait_send()
        for i in range(1, spans):
            to_span(i, t).wait_send()
        to_next(t).wait()


def shards(sizes, queries, keys_values, latents, out_weight, gate_table, level_index, pair_window):
    sections, spans, mps = sizes
    tokens, width = queries.shape[1:]
    rows, model = latents.shape[1:]
    heads = width // HD
    owners = spans * mps
    blocks = BLOCKS
    piece = rows // blocks
    group = owners * piece
    stat_rows = -(-heads // 8) * 8
    chunk = CHUNK if model % CHUNK == 0 else HD
    steps = blocks * (model // chunk)
    bf16, f32 = jnp.bfloat16, jnp.float32
    dma = pltpu.SemaphoreType.DMA
    hbm = pl.BlockSpec(memory_space=pltpu.HBM)
    return pl.pallas_call(
        functools.partial(fused, sections, spans, mps, blocks, chunk, LAG_MP, LAG_SPAN, LATE_STEP),
        out_shape=jax.ShapeDtypeStruct(latents.shape, bf16),
        in_specs=[hbm, hbm, hbm, hbm, hbm, hbm, hbm],
        out_specs=hbm,
        scratch_shapes=[
            pltpu.VMEM((owners, rows, width), bf16),
            pltpu.VMEM((2, tokens, width), bf16),
            pltpu.VMEM((rows, model), bf16),
            pltpu.VMEM(out_weight.shape, bf16),
            pltpu.VMEM(gate_table.shape, f32),
            pltpu.VMEM((2, blocks, owners, piece, width), bf16),
            pltpu.VMEM((2, blocks, heads, group, HD), bf16),
            pltpu.VMEM((2, blocks, heads, group, HD), bf16),
            pltpu.VMEM((2, blocks, stat_rows, group), f32),
            pltpu.VMEM((2, blocks, LANES, group), f32),
            pltpu.VMEM((blocks, group, width), f32),
            pltpu.VMEM((blocks, group, LANES), f32),
            pltpu.VMEM((blocks, 2 * group, LANES), f32),
            pltpu.VMEM((blocks, mps, spans, piece, width), bf16),
            pltpu.VMEM((steps, spans, piece, chunk), f32),
            pltpu.VMEM((mps - 1, steps, spans, piece, chunk), bf16),
            pltpu.VMEM((mps - 1, steps, spans, piece, chunk), bf16),
            pltpu.VMEM((spans - 1, steps, piece, chunk), bf16),
            pltpu.VMEM((spans - 1, steps, piece, chunk), bf16),
            pltpu.VMEM((steps, piece, chunk), bf16),
            pltpu.SMEM(level_index.shape, jnp.int32),
            pltpu.SMEM(pair_window.shape, jnp.int32),
            dma((7,)),
            dma((2, blocks, heads)), dma((2, blocks, heads)),
            dma((2, blocks, heads)), dma((2, blocks, heads)),
            dma((2, blocks)), dma((2, blocks)),
            dma((mps - 1, steps)), dma((mps - 1, steps)),
            dma((spans - 1, steps)), dma((spans - 1, steps)),
            dma((steps,)), dma((steps,)),
            pltpu.SemaphoreType.REGULAR,
        ],
        compiler_params=pltpu.CompilerParams(
            collective_id=0, has_side_effects=True, vmem_limit_bytes=60 * 1024 * 1024
        ),
    )(level_index, pair_window, queries.reshape(owners, rows, width), keys_values, latents, out_weight, gate_table)


def solution(mesh):
    sizes = (mesh.shape["section"], mesh.shape["span"], mesh.shape["mp"])
    in_specs = (
        P(("group", "section"), None, ("span", "mp")),
        P(None, ("group", "section"), None, ("span", "mp")),
        P(("group", "section"), ("span", "mp"), None),
        P(("span", "mp"), None),
        P(),
        P(("group", "section")),
        P("group"),
    )
    out_specs = P(("group", "section"), ("span", "mp"), None)
    return jax.shard_map(
        functools.partial(shards, sizes), mesh=mesh, in_specs=in_specs, out_specs=out_specs,
        check_vma=False,
    )
```
